512 devices in a mesh: pb: 32 (over x, z), ao: 16 (over y, core).
Axes of the slice: x: 4, y: 8, z: 8, core: 2. Of those that a mesh axis runs over, the one named last changes fastest.
Arguments:
- queries: bfloat16 [32768, 128], P('pb'), may hold values from -4 to 4
- centres: bfloat16 [32768, 128], P(('pb', 'ao')), may hold values from -4 to 4
- coefs: bfloat16 [32768, 4096], P('pb', 'ao'), may hold values from -3 to 3
- pattern: int32 [32, 5], replicated, may hold values from 0 to 1, as said below
Outputs:
- scores: bfloat16 [32768, 4096], P('pb', 'ao')
The draws below stay inside these ranges and needn't reach their ends.
Inputs may be any that keep to these rules, and one draw needn't show every extreme that they name: pattern[i, j] tells whether query block i lists centre block i + j - 2; it is 0 where that block lies outside 0 to 31, and 1 for j = 2.
All inputs are finite; a program needn't handle non-finite values.
Results may differ from the reference program's by a relative error of at most 0.0049.
Values may be sent and summed in bfloat16 or wider, within the bound.
A program may use at most 64 MiB of HBM per device.

```python
import math
import jax
import jax.numpy as jnp
from jax import lax

F = 128
OUT = 4096
CBS = 1024
HALF = 2
QDEV = 1024
NQB = 32
BAND = 5
NQ = 32768
NC = 32768


def coordinates(key, count, salt):
    base = jax.random.fold_in(key, salt)
    values = jnp.clip(jax.random.normal(jax.random.fold_in(base, 1), (count, F), jnp.float32), -4.0, 4.0)
    spread = jnp.exp(jax.random.uniform(jax.random.fold_in(base, 2), (count, 1), jnp.float32, math.log(0.5), 0.0))
    return (values * spread).astype(jnp.bfloat16)


def draw_queries(key, part):
    return coordinates(key, NQ, 101)


def draw_centres(key, part):
    return coordinates(key, NC, 202)


def draw_pattern(key, part):
    level = jax.random.randint(jax.random.fold_in(key, 303), (NQB, 1), 1, 4)
    coin = jax.random.randint(jax.random.fold_in(key, 304), (NQB, BAND), 0, 3)
    listed = (coin < level).astype(jnp.int32)
    block_ids = jnp.arange(NQB, dtype=jnp.int32)[:, None]
    shifts = jnp.arange(BAND, dtype=jnp.int32)[None, :] - HALF
    target = block_ids + shifts
    inside = (target >= 0) & (target < NQB)
    result = jnp.where(shifts == 0, 1, jnp.where(inside, listed, 0))
    return result.astype(jnp.int32)


def block_scale(own_key, shape, pieces, low, high):
    factor_of, own = 1.0, jax.random.fold_in(own_key, 6)
    for dim, shards_of in pieces:
        draws = jnp.exp(jax.random.uniform(jax.random.fold_in(own, dim), (shards_of,), jnp.float32, low / len(pieces), high / len(pieces)))
        factor_of = factor_of * jnp.repeat(draws, shape[dim] // shards_of).reshape([-1 if axis == dim else 1 for axis in range(len(shape))])
    return factor_of


def gaussian(stream_key, shape, scale, limit, split=(), kind=jnp.bfloat16):
    level = block_scale(stream_key, shape, split, -0.22, 0.18) if split else 1.0
    values = jax.random.normal(stream_key, shape, jnp.float32) * scale * level
    return jnp.minimum(jnp.maximum(values, -limit), limit).astype(kind)


def setup_inputs(seed: int = 0) -> dict:
    splits = jax.random.split(jax.random.key(seed), 5)
    queries = draw_queries(jax.random.fold_in(splits[4], 71), 0)
    centres = draw_centres(jax.random.fold_in(splits[4], 71), 0)
    coefs = gaussian(splits[2], (NC, OUT), 0.5, 3.0, ((0, 32), (1, 16)))
    pattern = draw_pattern(jax.random.fold_in(splits[4], 71), 0)
    return dict(queries=queries, centres=centres, coefs=coefs, pattern=pattern)


RADIUS_FACTOR = 1.3

def wendland_block(query_rows, query_norm, centre_rows):
    centre_wide = centre_rows.astype(jnp.float32)
    centre_norm = lax.optimization_barrier(jnp.sum(centre_wide * centre_wide, axis=1))[None, :]
    cross = jnp.dot(query_rows, centre_rows.T, preferred_element_type=jnp.float32)
    dist = jnp.sqrt(query_norm + centre_norm - 2.0 * cross)
    scaled = dist / (RADIUS_FACTOR * math.sqrt(query_rows.shape[1]))
    inner = jnp.maximum(1.0 - scaled, 0.0)
    return inner * inner * inner * inner * (4.0 * scaled + 1.0)

def reference(queries, centres, coefs, pattern):

    def one_block(block_index):
        query_rows = lax.dynamic_slice_in_dim(queries, (block_index * QDEV).astype(jnp.int32), QDEV, 0)
        query_wide = query_rows.astype(jnp.float32)
        query_norm = lax.optimization_barrier(jnp.sum(query_wide * query_wide, axis=1))[:, None]

        def add_block(offset, accumulated):
            offset = jnp.asarray(offset).astype(jnp.int32)
            target = block_index + offset - HALF
            clamped = jnp.clip(target, 0, NQB - 1).astype(jnp.int32)
            centre_rows = lax.dynamic_slice_in_dim(centres, clamped * CBS, CBS, 0)
            coef_rows = lax.dynamic_slice_in_dim(coefs, clamped * CBS, CBS, 0)
            listed = pattern[block_index, offset]

            def compute(current):
                kern = (wendland_block(query_rows, query_norm, centre_rows) * listed.astype(jnp.float32)).astype(jnp.bfloat16)
                return current + jnp.dot(kern, coef_rows, preferred_element_type=jnp.float32)
            return lax.cond(listed > 0, compute, lambda current: current, accumulated)
        accumulated = lax.fori_loop(0, BAND, add_block, jnp.zeros((QDEV, OUT), jnp.float32))
        return accumulated.astype(jnp.bfloat16)
    blocks = lax.map(one_block, jnp.arange(NQB, dtype=jnp.int32))
    return blocks.reshape(NQ, OUT)
```

```python
import functools
import math

import jax
import jax.numpy as jnp
from jax import lax
from jax.experimental import pallas as pl
from jax.experimental.pallas import tpu as pltpu
from jax.sharding import PartitionSpec as P

RADIUS_FACTOR = 1.3
MESH = pl.DeviceIdType.MESH
F32 = jnp.float32
BF16 = jnp.bfloat16

OFFSETS = (0, -1, 1, -2, 2)
GROUPS = ((0, 1), (1, 3), (3, 5))
CHUNKS = 4


def wendland(sq_dist, radius, high, low):
    clamped = jnp.maximum(sq_dist, 1e-30)
    inner = jnp.maximum(radius - clamped * lax.rsqrt(clamped), 0.0)
    square = inner * inner
    return ((square * square) * (high - low * inner)).astype(BF16)


def kernel(
    n_pb, n_ao,
    queries_hbm, centres_hbm, coefs_hbm, pattern_hbm, out_ref,
    queries, wide_queries, ones, centres, coefs, kern, total, pattern,
    local_sem, zs, zr, ys, yr, ss, sr, ks, kr,
):
    n_y = n_ao // 2
    half = n_y // 2
    n_q, features = queries.shape
    rows = centres.shape[2]
    per_y = 2 * rows
    block = n_y * per_y
    chunk = block // CHUNKS
    radius = RADIUS_FACTOR * math.sqrt(features)

    pb = lax.axis_index("pb")
    ao = lax.axis_index("ao")
    y = ao // 2
    core = ao % 2
    sibling = (pb, y * 2 + (1 - core))
    y_up = (pb, lax.rem(y + 1, n_y) * 2 + core)
    y_down = (pb, lax.rem(y + n_y - 1, n_y) * 2 + core)
    pb_up = (lax.rem(pb + 1, n_pb), ao)
    pb_down = (lax.rem(pb + n_pb - 1, n_pb), ao)

    barrier = pltpu.get_barrier_semaphore()
    for peer in (pb_up, pb_down, y_up, y_down, sibling):
        pl.semaphore_signal(barrier, inc=1, device_id=peer, device_id_type=MESH)

    own_centres = pltpu.make_async_copy(centres_hbm, centres.at[ao, 0], local_sem.at[0])
    own_coefs = pltpu.make_async_copy(coefs_hbm, coefs.at[0], local_sem.at[1])
    own_queries = pltpu.make_async_copy(queries_hbm, queries, local_sem.at[2])
    own_pattern = pltpu.make_async_copy(pattern_hbm, pattern, local_sem.at[3])
    own_centres.start()
    own_coefs.start()
    own_queries.start()
    own_pattern.start()
    own_centres.wait()
    own_coefs.wait()
    pl.semaphore_wait(barrier, 5)

    started = []

    def send(src, dst, send_sem, recv_sem, device):
        copy = pltpu.make_async_remote_copy(
            src_ref=src, dst_ref=dst, send_sem=send_sem, recv_sem=recv_sem,
            device_id=device, device_id_type=MESH,
        )
        copy.start()
        started.append(copy)

    def z_copy(direction, hop):
        src = 0 if hop == 0 else 1 + direction
        return (
            centres.at[ao, src], centres.at[ao, 1 + 2 * hop + direction],
            zs.at[direction, hop], zr.at[direction, hop], (pb_up, pb_down)[direction],
        )

    def coef_copy(direction, hop, part):
        src = 0 if hop == 0 else 1 + direction
        span = pl.ds(part * chunk, chunk)
        return (
            coefs.at[src, span], coefs.at[1 + 2 * hop + direction, span],
            ks.at[direction, hop, part], kr.at[direction, hop, part], (pb_up, pb_down)[direction],
        )

    def ring_view(group, owner, of_core):
        first, last = GROUPS[group]
        return centres.at[owner * 2 + of_core, pl.ds(first, last - first)]

    def owner_of(direction, hop):
        return lax.rem(y + n_y - hop, n_y) if direction == 0 else lax.rem(y + hop, n_y)

    def ring_copy(group, direction, hop):
        view = ring_view(group, owner_of(direction, hop), core)
        return (
            view, view, ys.at[group, direction, hop], yr.at[group, direction, hop],
            (y_up, y_down)[direction],
        )

    def sibling_copy(group, direction, hop, of_core):
        view = ring_view(group, owner_of(direction, hop), of_core)
        return (view, view, ss.at[group, direction, hop], sr.at[group, direction, hop], sibling)

    def arrived(args):
        src, dst, send_sem, recv_sem, device = args
        pltpu.make_async_remote_copy(
            src_ref=src, dst_ref=dst, send_sem=send_sem, recv_sem=recv_sem,
            device_id=device, device_id_type=MESH,
        ).wait_recv()

    def ring_arrived(group, direction, hop):
        view = ring_view(group, owner_of(direction, hop), core)
        arrived((view, view, ys.at[group, direction, hop - 1], yr.at[group, direction, hop - 1],
                 (y_up, y_down)[direction]))

    def start_own(group):
        send(*ring_copy(group, 0, 0))
        send(*ring_copy(group, 1, 0))
        send(*sibling_copy(group, 0, 0, core))

    def serve(group, hop):
        ring_arrived(group, 0, hop)
        if hop < half:
            send(*ring_copy(group, 0, hop))
        send(*sibling_copy(group, 0, hop, core))
        if hop < half:
            ring_arrived(group, 1, hop)
            if hop < half - 1:
                send(*ring_copy(group, 1, hop))
            send(*sibling_copy(group, 1, hop, core))

    def sibling_arrived(group, hop):
        arrived(sibling_copy(group, 0, hop, 1 - core))
        if 0 < hop < half:
            arrived(sibling_copy(group, 1, hop, 1 - core))

    for direction in (0, 1):
        send(*z_copy(direction, 0))
    start_own(0)
    for part in range(CHUNKS):
        for direction in (0, 1):
            send(*coef_copy(direction, 0, part))

    own_queries.wait()
    wide = queries[...].astype(F32)
    norm = jnp.sum(wide * wide, axis=1, keepdims=True)
    high = norm.astype(BF16).astype(F32)
    middle = (norm - high).astype(BF16).astype(F32)
    low = norm - high - middle
    lane = lax.broadcasted_iota(jnp.int32, (n_q, features), 1)
    pieces = jnp.where(lane == 0, high, jnp.where(lane == 1, middle, jnp.where(lane == 2, low, 0.0)))
    wide_queries[:, :features] = (-2.0 * wide).astype(BF16)
    wide_queries[:, features:] = pieces.astype(BF16)
    lane = lax.broadcasted_iota(jnp.int32, ones.shape, 1)
    ones[...] = jnp.where(lane < 3, 1.0, 0.0).astype(BF16)
    own_pattern.wait()

    def piece(slot, hop):
        if hop == half:
            pair = (y, owner_of(0, half))
        else:
            pair = (owner_of(0, hop), owner_of(1, hop))
        listed = pattern[pb, 2 + OFFSETS[slot]].astype(F32)
        top = listed * (5.0 / radius ** 4)
        slope = listed * (4.0 / radius ** 5)
        points = jnp.concatenate(
            [centres[owner * 2 + of_core, slot] for owner in pair for of_core in (0, 1)], axis=0
        )
        point_wide = points.astype(F32)
        square = point_wide * point_wide
        square_high = square.astype(BF16)
        square_low = (square - square_high.astype(F32)).astype(BF16)
        point_norm = lax.dot_general(
            jnp.ones((8, 2 * features), BF16), jnp.concatenate([square_high, square_low], axis=1),
            (((1,), (1,)), ((), ())), preferred_element_type=F32,
        )
        right = jnp.concatenate([points, ones[...]], axis=1)
        tile = n_q // 2

        @pl.loop(0, n_q // tile)
        def _(t):
            span = pl.ds(pl.multiple_of(t * tile, tile), tile)
            cross = lax.dot_general(
                wide_queries[span, :], right, (((1,), (1,)), ((), ())), preferred_element_type=F32
            )
            sq_dist = (cross.reshape(tile // 8, 8, 2 * per_y) + point_norm[None]).reshape(tile, 2 * per_y)
            value = wendland(sq_dist, radius, top, slope)
            for k, owner in enumerate(pair):
                kern[slot, span, pl.ds(pl.multiple_of(owner * per_y, per_y), per_y)] = (
                    value[:, k * per_y:(k + 1) * per_y]
                )

    def compute(group, hop):
        sibling_arrived(group, hop)
        if hop == half:
            sibling_arrived(group, 0)
        for slot in range(*GROUPS[group]):
            piece(slot, hop)

    def coefs_arrived(hop, part, forward):
        for direction in (0, 1):
            arrived(coef_copy(direction, hop, part))
            if forward:
                send(*coef_copy(direction, 1, part))

    def product(slot, first=0, last=CHUNKS):
        span = slice(first * chunk, last * chunk)
        return jnp.dot(kern[slot, :, span], coefs[slot, span, :], preferred_element_type=F32)

    serve(0, 1)
    for direction in (0, 1):
        arrived(z_copy(direction, 0))
        send(*z_copy(direction, 1))
    start_own(1)
    compute(0, 1)
    serve(0, 2)
    serve(1, 1)
    for direction in (0, 1):
        arrived(z_copy(direction, 1))
    start_own(2)
    compute(0, 2)
    serve(0, 3)
    serve(1, 2)
    compute(1, 1)
    serve(2, 1)
    serve(0, 4)
    compute(0, 3)
    serve(1, 3)
    serve(2, 2)
    compute(1, 2)
    serve(1, 4)
    compute(0, 4)
    serve(2, 3)
    total[...] = product(0)
    compute(1, 3)
    serve(2, 4)
    coefs_arrived(0, 0, True)
    coefs_arrived(0, 1, True)
    compute(1, 4)
    compute(2, 1)
    coefs_arrived(0, 2, True)
    compute(2, 2)
    coefs_arrived(0, 3, True)
    compute(2, 3)
    total[...] += product(1) + product(2)
    compute(2, 4)
    for part in range(CHUNKS):
        coefs_arrived(1, part, False)
        partial = product(3, part, part + 1) + product(4, part, part + 1)
        if part < CHUNKS - 1:
            total[...] += partial
        else:
            out_ref[...] = (total[...] + partial).astype(BF16)
    for copy in started:
        copy.wait_send()


def per_device(n_pb, n_ao, queries, centres, coefs, pattern):
    n_q, features = queries.shape
    n_c, columns = coefs.shape
    anywhere = pl.BlockSpec(memory_space=pl.ANY)
    half = n_ao // 4
    dma = pltpu.SemaphoreType.DMA
    return pl.pallas_call(
        functools.partial(kernel, n_pb, n_ao),
        out_shape=jax.ShapeDtypeStruct((n_q, columns), BF16),
        in_specs=[anywhere] * 4,
        out_specs=pl.BlockSpec(memory_space=pltpu.VMEM),
        scratch_shapes=[
            pltpu.VMEM((n_q, features), BF16),
            pltpu.VMEM((n_q, 2 * features), BF16),
            pltpu.VMEM((4 * centres.shape[0], features), BF16),
            pltpu.VMEM((n_ao, 5, centres.shape[0], features), BF16),
            pltpu.VMEM((5, n_c, columns), BF16),
            pltpu.VMEM((5, n_q, n_c), BF16),
            pltpu.VMEM((n_q, columns), F32),
            pltpu.SMEM(pattern.shape, jnp.int32),
            dma((4,)),
            dma((2, 2)), dma((2, 2)),
            dma((3, 2, half)), dma((3, 2, half)),
            dma((3, 2, half + 1)), dma((3, 2, half + 1)),
            dma((2, 2, CHUNKS)), dma((2, 2, CHUNKS)),
        ],
        compiler_params=pltpu.CompilerParams(
            collective_id=0, has_side_effects=True, vmem_limit_bytes=60 * 2 ** 20
        ),
    )(queries, centres, coefs, pattern)


def solution(mesh):
    in_specs = (P("pb", None), P(("pb", "ao"), None), P("pb", "ao"), P())
    out_specs = P("pb", "ao")
    return jax.shard_map(
        functools.partial(per_device, mesh.shape["pb"], mesh.shape["ao"]),
        mesh=mesh, in_specs=in_specs, out_specs=out_specs, check_vma=False,
    )
```

```python
import functools
import math

import jax
import jax.numpy as jnp
from jax import lax
from jax.experimental import pallas as pl
from jax.experimental.pallas import tpu as pltpu
from jax.sharding import PartitionSpec as P

RADIUS_FACTOR = 1.3
MESH = pl.DeviceIdType.MESH
F32 = jnp.float32
BF16 = jnp.bfloat16

OFFSETS = (0, -1, 1, -2, 2)
GROUPS = ((0, 1), (1, 3), (3, 5))
CHUNKS = 4


def wendland(sq_dist, radius, high, low):
    clamped = jnp.maximum(sq_dist, 1e-30)
    inner = jnp.maximum(radius - clamped * lax.rsqrt(clamped), 0.0)
    square = inner * inner
    return ((square * square) * (high - low * inner)).astype(BF16)


def kernel(
    n_pb, n_ao,
    queries_hbm, centres_hbm, coefs_hbm, pattern_hbm, out_ref,
    queries, wide_queries, ones, centres, coefs, kern, total, pattern,
    local_sem, zs, zr, ys, yr, ss, sr, ks, kr,
):
    n_y = n_ao // 2
    n_q, features = queries.shape
    rows = centres.shape[2]
    block = coefs.shape[1]
    chunk = block // CHUNKS
    share = n_y * rows
    radius = RADIUS_FACTOR * math.sqrt(features)

    pb = lax.axis_index("pb")
    ao = lax.axis_index("ao")
    y = ao // 2
    core = ao % 2
    sibling = (pb, y * 2 + (1 - core))
    steps = sorted(range(1, n_y), key=lambda d: min(d, n_y - d))

    def y_peer(d):
        return (pb, lax.rem(y + d, n_y) * 2 + core)

    def pb_peer(shift):
        return (lax.rem(pb + shift + n_pb, n_pb), ao)

    barrier = pltpu.get_barrier_semaphore()
    peers = [pb_peer(-shift) for shift in OFFSETS[1:]] + [sibling] + [y_peer(d) for d in steps]
    for peer in peers:
        pl.semaphore_signal(barrier, inc=1, device_id=peer, device_id_type=MESH)

    own_centres = pltpu.make_async_copy(centres_hbm, centres.at[y, 0], local_sem.at[0])
    own_coefs = pltpu.make_async_copy(coefs_hbm, coefs.at[0], local_sem.at[1])
    own_queries = pltpu.make_async_copy(queries_hbm, queries, local_sem.at[2])
    own_pattern = pltpu.make_async_copy(pattern_hbm, pattern, local_sem.at[3])
    own_centres.start()
    own_coefs.start()
    own_queries.start()
    own_pattern.start()

    def remote(src, dst, send_sem, recv_sem, device):
        return pltpu.make_async_remote_copy(
            src_ref=src, dst_ref=dst, send_sem=send_sem, recv_sem=recv_sem,
            device_id=device, device_id_type=MESH,
        )

    def z_copy(slot):
        return remote(
            centres.at[y, 0], centres.at[y, slot], zs.at[slot - 1], zr.at[slot - 1],
            pb_peer(-OFFSETS[slot]),
        )

    def coef_copy(direction, hop, part):
        src = 0 if hop == 0 else 1 + direction
        span = pl.ds(part * chunk, chunk)
        return remote(
            coefs.at[src, span], coefs.at[1 + 2 * hop + direction, span],
            ks.at[direction, hop, part], kr.at[direction, hop, part],
            pb_peer(1 if direction == 0 else -1),
        )

    def y_copy(group, d, arriving=False):
        first, last = GROUPS[group]
        owner = lax.rem(y + n_y - d, n_y) if arriving else y
        view = centres.at[owner, pl.ds(first, last - first)]
        return remote(view, view, ys.at[group, d - 1], yr.at[group, d - 1], y_peer(d))

    def kern_copy(slot, arriving=False):
        view = kern.at[1 - core if arriving else core, slot]
        return remote(view, view, ss.at[slot], sr.at[slot], sibling)

    def spread(group):
        for d in steps:
            y_copy(group, d).start()

    def gathered(group):
        for d in steps:
            y_copy(group, d, arriving=True).wait_recv()

    def forward(part):
        for direction in (0, 1):
            coef_copy(direction, 0, part).wait_recv()
            coef_copy(direction, 1, part).start()

    own_centres.wait()
    own_coefs.wait()
    pl.semaphore_wait(barrier, len(peers))

    for slot in range(1, 5):
        z_copy(slot).start()
    for part in range(CHUNKS):
        for direction in (0, 1):
            coef_copy(direction, 0, part).start()
    spread(0)

    own_queries.wait()
    wide = queries[...].astype(F32)
    norm = jnp.sum(wide * wide, axis=1, keepdims=True)
    high = norm.astype(BF16).astype(F32)
    middle = (norm - high).astype(BF16).astype(F32)
    low = norm - high - middle
    lane = lax.broadcasted_iota(jnp.int32, (n_q, features), 1)
    pieces = jnp.where(lane == 0, high, jnp.where(lane == 1, middle, jnp.where(lane == 2, low, 0.0)))
    wide_queries[:, :features] = (-2.0 * wide).astype(BF16)
    wide_queries[:, features:] = pieces.astype(BF16)
    lane = lax.broadcasted_iota(jnp.int32, ones.shape, 1)
    ones[...] = jnp.where(lane < 3, 1.0, 0.0).astype(BF16)
    total[...] = jnp.zeros_like(total)
    own_pattern.wait()

    for group in (1, 2):
        for slot in range(*GROUPS[group]):
            z_copy(slot).wait_recv()
        spread(group)
    gathered(0)

    def evaluate(slot):
        place = 2 + jnp.where(slot % 2 == 1, -1, 1) * ((slot + 1) // 2)
        listed = pattern[place, pb].astype(F32)
        top = listed * (5.0 / radius ** 4)
        slope = listed * (4.0 / radius ** 5)
        points = centres[:, slot].reshape(share, features)
        point_wide = points.astype(F32)
        square = point_wide * point_wide
        square_high = square.astype(BF16)
        square_low = (square - square_high.astype(F32)).astype(BF16)
        point_norm = lax.dot_general(
            jnp.ones((8, 2 * features), BF16), jnp.concatenate([square_high, square_low], axis=1),
            (((1,), (1,)), ((), ())), preferred_element_type=F32,
        )
        right = jnp.concatenate([points, ones[...]], axis=1)
        tile = n_q // 2

        @pl.loop(0, n_q // tile)
        def _(t):
            span = pl.ds(pl.multiple_of(t * tile, tile), tile)
            cross = lax.dot_general(
                wide_queries[span, :], right, (((1,), (1,)), ((), ())), preferred_element_type=F32
            )
            sq_dist = (cross.reshape(tile // 8, 8, share) + point_norm[None]).reshape(tile, share)
            kern[core, slot, span, :] = wendland(sq_dist, radius, top, slope)

    def product(slot, first, n_parts):
        owners = n_y // CHUNKS * n_parts
        start = first * (n_y // CHUNKS)
        columns = pl.ds(pl.multiple_of(start * rows, 128), owners * rows)
        left = jnp.concatenate([kern[c, slot, :, columns] for c in (0, 1)], axis=1)
        right = jnp.concatenate(
            [
                coefs[slot, pl.ds(pl.multiple_of((start + k) * 2 * rows + c * rows, rows), rows), :]
                for c in (0, 1) for k in range(owners)
            ],
            axis=0,
        )
        return jnp.dot(left, right, preferred_element_type=F32)

    @pl.loop(0, 5)
    def _(slot):
        @pl.when(slot == 1)
        def _():
            forward(0)
            gathered(1)
            forward(1)

        @pl.when(slot == 2)
        def _():
            forward(2)

        @pl.when(slot == 3)
        def _():
            forward(3)
            gathered(2)

        evaluate(slot)

        @pl.when(slot > 0)
        def _():
            kern_copy(slot - 1).start()

        @pl.when(slot > 1)
        def _():
            kern_copy(slot - 2, arriving=True).wait_recv()
            total[...] += product(slot - 2, 0, CHUNKS)

    kern_copy(4).start()
    kern_copy(3, arriving=True).wait_recv()
    kern_copy(4, arriving=True).wait_recv()

    @pl.loop(0, CHUNKS)
    def _(part):
        for direction in (0, 1):
            coef_copy(direction, 1, part).wait_recv()
        total[...] += product(3, part, 1) + product(4, part, 1)

    out_ref[...] = total[...].astype(BF16)

    for slot in range(1, 5):
        z_copy(slot).wait_send()
    for group in range(3):
        for d in steps:
            y_copy(group, d).wait_send()
    for part in range(CHUNKS):
        for direction in (0, 1):
            for hop in (0, 1):
                coef_copy(direction, hop, part).wait_send()
    for slot in range(5):
        kern_copy(slot).wait_send()


def per_device(n_pb, n_ao, queries, centres, coefs, pattern):
    n_q, features = queries.shape
    n_c, columns = coefs.shape
    rows = centres.shape[0]
    in_hbm = pl.BlockSpec(memory_space=pltpu.HBM)
    n_y = n_ao // 2
    dma = pltpu.SemaphoreType.DMA
    return pl.pallas_call(
        functools.partial(kernel, n_pb, n_ao),
        out_shape=jax.ShapeDtypeStruct((n_q, columns), BF16),
        in_specs=[in_hbm] * 4,
        out_specs=pl.BlockSpec(memory_space=pltpu.VMEM),
        scratch_shapes=[
            pltpu.VMEM((n_q, features), BF16),
            pltpu.VMEM((n_q, 2 * features), BF16),
            pltpu.VMEM((n_y * rows, features), BF16),
            pltpu.VMEM((n_y, 5, rows, features), BF16),
            pltpu.VMEM((5, n_c, columns), BF16),
            pltpu.VMEM((2, 5, n_q, n_c // 2), BF16),
            pltpu.VMEM((n_q, columns), F32),
            pltpu.SMEM(pattern.shape[::-1], jnp.int32),
            dma((4,)),
            dma((4,)), dma((4,)),
            dma((3, n_y - 1)), dma((3, n_y - 1)),
            dma((5,)), dma((5,)),
            dma((2, 2, CHUNKS)), dma((2, 2, CHUNKS)),
        ],
        compiler_params=pltpu.CompilerParams(
            collective_id=0, has_side_effects=True, vmem_limit_bytes=36 * 2 ** 20
        ),
    )(queries, centres, coefs, pattern.T)


def solution(mesh):
    in_specs = (P("pb", None), P(("pb", "ao"), None), P("pb", "ao"), P())
    out_specs = P("pb", "ao")
    return jax.shard_map(
        functools.partial(per_device, mesh.shape["pb"], mesh.shape["ao"]),
        mesh=mesh, in_specs=in_specs, out_specs=out_specs, check_vma=False,
    )
```

```python
import functools
import math

import jax
import jax.numpy as jnp
from jax import lax
from jax.experimental import pallas as pl
from jax.experimental.pallas import tpu as pltpu
from jax.sharding import PartitionSpec as P

RADIUS_FACTOR = 1.3
MESH = pl.DeviceIdType.MESH
F32 = jnp.float32
BF16 = jnp.bfloat16

OFFSETS = (0, -1, 1, -2, 2)
GROUPS = ((0, 1), (1, 3), (3, 5))
CHUNKS = 4


def wendland(sq_dist, radius, high, low):
    clamped = jnp.maximum(sq_dist, 1e-30)
    inner = jnp.maximum(radius - clamped * lax.rsqrt(clamped), 0.0)
    square = inner * inner
    return ((square * square) * (high - low * inner)).astype(BF16)


def kernel(
    n_pb, n_ao,
    queries_hbm, centres_hbm, coefs_hbm, pattern_hbm, out_ref,
    queries, wide_queries, ones, centres, coefs, kern, total, pattern,
    local_sem, ready, far, zs, zr, ys, yr, ss, sr, ks, kr,
):
    n_y = n_ao // 2
    n_q, features = queries.shape
    rows = centres.shape[2]
    block = coefs.shape[1]
    chunk = block // CHUNKS
    share = n_y * rows
    radius = RADIUS_FACTOR * math.sqrt(features)

    pb = lax.axis_index("pb")
    ao = lax.axis_index("ao")
    y = ao // 2
    core = ao % 2
    sibling = (pb, y * 2 + (1 - core))
    steps = sorted(range(1, n_y), key=lambda d: min(d, n_y - d))

    def y_peer(d):
        return (pb, lax.rem(y + d, n_y) * 2 + core)

    def pb_peer(shift):
        return (lax.rem(pb + shift + n_pb, n_pb), ao)

    has_below = pb > 0
    has_above = pb < n_pb - 1
    sends = (has_above, has_below)
    receives = (has_below, has_above)

    barrier = pltpu.get_barrier_semaphore()
    for peer in (y_peer(1), y_peer(n_y - 1), sibling):
        pl.semaphore_signal(barrier, inc=1, device_id=peer, device_id_type=MESH)

    @pl.when(has_below)
    def _():
        pl.semaphore_signal(barrier, inc=1, device_id=pb_peer(-1), device_id_type=MESH)

    own_centres = pltpu.make_async_copy(centres_hbm, centres.at[y, 0], local_sem.at[0])
    own_coefs = pltpu.make_async_copy(coefs_hbm, coefs.at[0], local_sem.at[1])
    own_queries = pltpu.make_async_copy(queries_hbm, queries, local_sem.at[2])
    own_pattern = pltpu.make_async_copy(pattern_hbm, pattern, local_sem.at[3])
    own_centres.start()
    own_coefs.start()
    own_queries.start()
    own_pattern.start()

    def remote(src, dst, send_sem, recv_sem, device):
        return pltpu.make_async_remote_copy(
            src_ref=src, dst_ref=dst, send_sem=send_sem, recv_sem=recv_sem,
            device_id=device, device_id_type=MESH,
        )

    def z_copy(direction, hop):
        src = 0 if hop == 0 else 1 + direction
        return remote(
            centres.at[y, src], centres.at[y, 1 + 2 * hop + direction],
            zs.at[direction, hop], zr.at[direction, hop], pb_peer(1 - 2 * direction),
        )

    def coef_copy(direction, hop, part):
        src = 0 if hop == 0 else 1 + direction
        span = pl.ds(part * chunk, chunk)
        return remote(
            coefs.at[src, span], coefs.at[1 + 2 * hop + direction, span],
            ks.at[direction, hop, part], kr.at[direction, hop, part], pb_peer(1 - 2 * direction),
        )

    def y_copy(group, d, arriving=False):
        first, last = GROUPS[group]
        owner = lax.rem(y + n_y - d, n_y) if arriving else y
        view = centres.at[owner, pl.ds(first, last - first)]
        return remote(view, view, ys.at[group, d - 1], yr.at[group, d - 1], y_peer(d))

    def kern_copy(slot, arriving=False):
        view = kern.at[1 - core if arriving else core, slot]
        return remote(view, view, ss.at[slot], sr.at[slot], sibling)

    def spread(group):
        for d in steps:
            y_copy(group, d).start()

    def gathered(group):
        for d in steps:
            y_copy(group, d, arriving=True).wait_recv()

    def forward(part):
        for direction in (0, 1):
            coef_copy(direction, 0, part).wait_recv()

            @pl.when(sends[direction])
            def _():
                coef_copy(direction, 1, part).start()

    for direction in (0, 1):
        @pl.when(jnp.logical_not(receives[direction]))
        def _():
            for hop in (0, 1):
                slot = 1 + 2 * hop + direction
                pltpu.make_async_copy(centres_hbm, centres.at[y, slot], zr.at[direction, hop]).start()
                for part in range(CHUNKS):
                    span = pl.ds(part * chunk, chunk)
                    pltpu.make_async_copy(
                        coefs_hbm.at[span], coefs.at[slot, span], kr.at[direction, hop, part]
                    ).start()

    own_centres.wait()
    own_coefs.wait()
    pl.semaphore_wait(barrier, 3 + has_above.astype(jnp.int32))

    @pl.when(has_above)
    def _():
        pl.semaphore_signal(ready, inc=1, device_id=pb_peer(1), device_id_type=MESH)
        z_copy(0, 0).start()
        for part in range(CHUNKS // 2):
            coef_copy(0, 0, part).start()

    y_copy(0, 1).start()
    y_copy(0, n_y - 1).start()

    @pl.when(has_below)
    def _():
        pl.semaphore_wait(ready, 1)
        z_copy(1, 0).start()
        for part in range(CHUNKS // 2):
            coef_copy(1, 0, part).start()

    for d in range(2, n_y // 2 + 1):
        pl.semaphore_signal(far.at[0, d - 2], inc=1, device_id=y_peer(n_y - 1), device_id_type=MESH)
        if d < n_y - d:
            pl.semaphore_signal(far.at[1, d - 2], inc=1, device_id=y_peer(1), device_id_type=MESH)
        pl.semaphore_wait(far.at[0, d - 2], 1)
        y_copy(0, d).start()
        if d < n_y - d:
            pl.semaphore_wait(far.at[1, d - 2], 1)
            y_copy(0, n_y - d).start()

    own_queries.wait()
    wide = queries[...].astype(F32)
    norm = jnp.sum(wide * wide, axis=1, keepdims=True)
    high = norm.astype(BF16).astype(F32)
    middle = (norm - high).astype(BF16).astype(F32)
    low = norm - high - middle
    lane = lax.broadcasted_iota(jnp.int32, (n_q, features), 1)
    pieces = jnp.where(lane == 0, high, jnp.where(lane == 1, middle, jnp.where(lane == 2, low, 0.0)))
    wide_queries[:, :features] = (-2.0 * wide).astype(BF16)
    wide_queries[:, features:] = pieces.astype(BF16)
    lane = lax.broadcasted_iota(jnp.int32, ones.shape, 1)
    ones[...] = jnp.where(lane < 3, 1.0, 0.0).astype(BF16)
    total[...] = jnp.zeros_like(total)
    own_pattern.wait()

    for hop in (0, 1):
        for direction in (0, 1):
            z_copy(direction, hop).wait_recv()
            if hop == 0:
                @pl.when(sends[direction])
                def _():
                    z_copy(direction, 1).start()
                    for part in range(CHUNKS // 2, CHUNKS):
                        coef_copy(direction, 0, part).start()
        spread(hop + 1)
    gathered(0)

    def evaluate(slot):
        place = 2 + jnp.where(slot % 2 == 1, -1, 1) * ((slot + 1) // 2)
        listed = pattern[place, pb].astype(F32)
        top = listed * (5.0 / radius ** 4)
        slope = listed * (4.0 / radius ** 5)
        points = centres[:, slot].reshape(share, features)
        point_wide = points.astype(F32)
        square = point_wide * point_wide
        square_high = square.astype(BF16)
        square_low = (square - square_high.astype(F32)).astype(BF16)
        point_norm = lax.dot_general(
            jnp.ones((8, 2 * features), BF16), jnp.concatenate([square_high, square_low], axis=1),
            (((1,), (1,)), ((), ())), preferred_element_type=F32,
        )
        right = jnp.concatenate([points, ones[...]], axis=1)
        tile = n_q // 2

        @pl.loop(0, n_q // tile)
        def _(t):
            span = pl.ds(pl.multiple_of(t * tile, tile), tile)
            cross = lax.dot_general(
                wide_queries[span, :], right, (((1,), (1,)), ((), ())), preferred_element_type=F32
            )
            sq_dist = (cross.reshape(tile // 8, 8, share) + point_norm[None]).reshape(tile, share)
            kern[core, slot, span, :] = wendland(sq_dist, radius, top, slope)

    def product(slot, first, n_parts):
        owners = n_y // CHUNKS * n_parts
        start = first * (n_y // CHUNKS)
        columns = pl.ds(pl.multiple_of(start * rows, 128), owners * rows)
        left = jnp.concatenate([kern[c, slot, :, columns] for c in (0, 1)], axis=1)
        right = jnp.concatenate(
            [
                coefs[slot, pl.ds(pl.multiple_of((start + k) * 2 * rows + c * rows, rows), rows), :]
                for c in (0, 1) for k in range(owners)
            ],
            axis=0,
        )
        return jnp.dot(left, right, preferred_element_type=F32)

    @pl.loop(0, 5)
    def _(slot):
        @pl.when(slot == 1)
        def _():
            forward(0)
            gathered(1)
            forward(1)

        @pl.when(slot == 2)
        def _():
            forward(2)

        @pl.when(slot == 3)
        def _():
            forward(3)
            gathered(2)

        evaluate(slot)

        @pl.when(slot > 0)
        def _():
            kern_copy(slot - 1).start()

        @pl.when(slot > 1)
        def _():
            kern_copy(slot - 2, arriving=True).wait_recv()
            total[...] += product(slot - 2, 0, CHUNKS)

    kern_copy(4).start()
    kern_copy(3, arriving=True).wait_recv()
    kern_copy(4, arriving=True).wait_recv()

    def last_products(part):
        for direction in (0, 1):
            coef_copy(direction, 1, part).wait_recv()
        return total[...] + (product(3, part, 1) + product(4, part, 1))

    @pl.loop(0, CHUNKS - 1)
    def _(part):
        total[...] = last_products(part)

    out_ref[...] = last_products(CHUNKS - 1).astype(BF16)

    for direction in (0, 1):
        @pl.when(sends[direction])
        def _():
            for hop in (0, 1):
                z_copy(direction, hop).wait_send()
                for part in range(CHUNKS):
                    coef_copy(direction, hop, part).wait_send()

    for group in range(3):
        for d in steps:
            y_copy(group, d).wait_send()
    for slot in range(5):
        kern_copy(slot).wait_send()


def per_device(n_pb, n_ao, queries, centres, coefs, pattern):
    n_q, features = queries.shape
    n_c, columns = coefs.shape
    rows = centres.shape[0]
    in_hbm = pl.BlockSpec(memory_space=pltpu.HBM)
    n_y = n_ao // 2
    dma = pltpu.SemaphoreType.DMA
    return pl.pallas_call(
        functools.partial(kernel, n_pb, n_ao),
        out_shape=jax.ShapeDtypeStruct((n_q, columns), BF16),
        in_specs=[in_hbm] * 4,
        out_specs=pl.BlockSpec(memory_space=pltpu.VMEM),
        scratch_shapes=[
            pltpu.VMEM((n_q, features), BF16),
            pltpu.VMEM((n_q, 2 * features), BF16),
            pltpu.VMEM((n_y * rows, features), BF16),
            pltpu.VMEM((n_y, 5, rows, features), BF16),
            pltpu.VMEM((5, n_c, columns), BF16),
            pltpu.VMEM((2, 5, n_q, n_c // 2), BF16),
            pltpu.VMEM((n_q, columns), F32),
            pltpu.SMEM(pattern.shape[::-1], jnp.int32),
            dma((4,)),
            pltpu.SemaphoreType.REGULAR,
            pltpu.SemaphoreType.REGULAR((2, n_y // 2 - 1)),
            dma((2, 2)), dma((2, 2)),
            dma((3, n_y - 1)), dma((3, n_y - 1)),
            dma((5,)), dma((5,)),
            dma((2, 2, CHUNKS)), dma((2, 2, CHUNKS)),
        ],
        compiler_params=pltpu.CompilerParams(
            collective_id=0, has_side_effects=True, vmem_limit_bytes=36 * 2 ** 20
        ),
    )(*[pltpu.with_memory_space_constraint(x, pltpu.HBM) for x in (queries, centres, coefs, pattern.T)])


def solution(mesh):
    in_specs = (P("pb", None), P(("pb", "ao"), None), P("pb", "ao"), P())
    out_specs = P("pb", "ao")
    return jax.shard_map(
        functools.partial(per_device, mesh.shape["pb"], mesh.shape["ao"]),
        mesh=mesh, in_specs=in_specs, out_specs=out_specs, check_vma=False,
    )
```

```python
import functools
import math

import jax
import jax.numpy as jnp
from jax import lax
from jax.experimental import pallas as pl
from jax.experimental.pallas import tpu as pltpu
from jax.sharding import PartitionSpec as P

RADIUS_FACTOR = 1.3
MESH = pl.DeviceIdType.MESH
F32 = jnp.float32
BF16 = jnp.bfloat16

OFFSETS = (0, -1, 1, -2, 2)
CHUNKS = 4


def wendland(sq_dist, radius, high, low):
    clamped = jnp.maximum(sq_dist, 1e-30)
    inner = jnp.maximum(radius - clamped * lax.rsqrt(clamped), 0.0)
    square = inner * inner
    return ((square * square) * (high - low * inner)).astype(BF16)


def kernel(
    n_pb, n_ao,
    queries_hbm, centres_hbm, coefs_hbm, pattern_hbm, out_ref,
    queries, wide_queries, ones, centres, coefs, kern, total, pattern,
    local_sem, ready, far, zs, zr, ys, yr, ss, sr, ks, kr,
):
    n_y = n_ao // 2
    n_q, features = queries.shape
    rows = centres.shape[2]
    block = coefs.shape[1]
    chunk = block // CHUNKS
    share = n_y * rows
    half = n_q // 2
    radius = RADIUS_FACTOR * math.sqrt(features)

    pb = lax.axis_index("pb")
    ao = lax.axis_index("ao")
    y = ao // 2
    core = ao % 2
    sibling = (pb, y * 2 + (1 - core))
    def y_peer(d):
        return (pb, lax.rem(y + d, n_y) * 2 + core)

    def pb_peer(shift):
        return (lax.rem(pb + shift + n_pb, n_pb), ao)

    has_below = pb > 0
    has_above = pb < n_pb - 1
    sends = (has_above, has_below)
    receives = (has_below, has_above)

    barrier = pltpu.get_barrier_semaphore()
    for peer in (y_peer(1), y_peer(n_y - 1), sibling):
        pl.semaphore_signal(barrier, inc=1, device_id=peer, device_id_type=MESH)

    @pl.when(has_below)
    def _():
        pl.semaphore_signal(barrier, inc=1, device_id=pb_peer(-1), device_id_type=MESH)

    own_centres = pltpu.make_async_copy(centres_hbm, centres.at[y, 0], local_sem.at[0])
    own_coefs = pltpu.make_async_copy(coefs_hbm, coefs.at[0], local_sem.at[1])
    own_queries = pltpu.make_async_copy(queries_hbm, queries, local_sem.at[2])
    own_pattern = pltpu.make_async_copy(pattern_hbm, pattern, local_sem.at[3])
    own_centres.start()
    own_coefs.start()
    own_queries.start()
    own_pattern.start()

    def remote(src, dst, send_sem, recv_sem, device):
        return pltpu.make_async_remote_copy(
            src_ref=src, dst_ref=dst, send_sem=send_sem, recv_sem=recv_sem,
            device_id=device, device_id_type=MESH,
        )

    def z_copy(direction, hop):
        src = 0 if hop == 0 else 1 + direction
        return remote(
            centres.at[y, src], centres.at[y, 1 + 2 * hop + direction],
            zs.at[direction, hop], zr.at[direction, hop], pb_peer(1 - 2 * direction),
        )

    def coef_copy(direction, hop, part):
        src = 0 if hop == 0 else 1 + direction
        span = pl.ds(part * chunk, chunk)
        return remote(
            coefs.at[src, span], coefs.at[1 + 2 * hop + direction, span],
            ks.at[direction, hop, part], kr.at[direction, hop, part], pb_peer(1 - 2 * direction),
        )

    def y_copy(slot, direction, distance, arriving=False):
        behind = distance if arriving else (0 if distance < 3 else 2)
        hops = distance if distance < 3 else distance - 2
        sign = 1 - 2 * direction
        view = centres.at[lax.rem(y + n_y - sign * behind, n_y), slot]
        return remote(
            view, view, ys.at[slot, direction, distance - 1], yr.at[slot, direction, distance - 1],
            y_peer(n_y + sign * hops),
        )

    def farthest(slot, direction):
        return n_y // 2 if direction == slot % 2 else n_y // 2 - 1

    def kern_copy(slot, tile, arriving=False):
        view = kern.at[1 - core if arriving else core, slot, pl.ds(pl.multiple_of(tile * half, half), half)]
        return remote(view, view, ss.at[slot, tile], sr.at[slot, tile], sibling)

    def kern_arrived(slot):
        for tile in (0, 1):
            kern_copy(slot, tile, arriving=True).wait_recv()

    def spread(slot, distance):
        for direction in (0, 1):
            y_copy(slot, direction, distance).start()

    def relay(slot):
        for direction in (0, 1):
            y_copy(slot, direction, 2, arriving=True).wait_recv()
            for distance in range(3, farthest(slot, direction) + 1):
                y_copy(slot, direction, distance).start()

    def gathered(slot):
        for direction in (0, 1):
            for distance in range(1, farthest(slot, direction) + 1):
                if distance != 2:
                    y_copy(slot, direction, distance, arriving=True).wait_recv()

    def forward(part):
        for direction in (0, 1):
            coef_copy(direction, 0, part).wait_recv()

            @pl.when(sends[direction])
            def _():
                coef_copy(direction, 1, part).start()

    for direction in (0, 1):
        @pl.when(jnp.logical_not(receives[direction]))
        def _():
            for hop in (0, 1):
                slot = 1 + 2 * hop + direction
                pltpu.make_async_copy(centres_hbm, centres.at[y, slot], zr.at[direction, hop]).start()
                for part in range(CHUNKS):
                    span = pl.ds(part * chunk, chunk)
                    pltpu.make_async_copy(
                        coefs_hbm.at[span], coefs.at[slot, span], kr.at[direction, hop, part]
                    ).start()

    own_centres.wait()
    own_coefs.wait()
    pl.semaphore_wait(barrier, 3 + has_above.astype(jnp.int32))

    @pl.when(has_above)
    def _():
        pl.semaphore_signal(ready, inc=1, device_id=pb_peer(1), device_id_type=MESH)
        z_copy(0, 0).start()
        for part in range(CHUNKS // 2):
            coef_copy(0, 0, part).start()

    spread(0, 1)
    for direction in (0, 1):
        pl.semaphore_signal(
            far.at[direction], inc=1, device_id=y_peer(n_y - 1 + 2 * direction), device_id_type=MESH
        )

    @pl.when(has_below)
    def _():
        pl.semaphore_wait(ready, 1)
        z_copy(1, 0).start()
        for part in range(CHUNKS // 2):
            coef_copy(1, 0, part).start()

    for direction in (0, 1):
        pl.semaphore_wait(far.at[direction], 1)
    spread(0, 2)

    own_queries.wait()
    wide = queries[...].astype(F32)
    norm = jnp.sum(wide * wide, axis=1, keepdims=True)
    high = norm.astype(BF16).astype(F32)
    middle = (norm - high).astype(BF16).astype(F32)
    low = norm - high - middle
    lane = lax.broadcasted_iota(jnp.int32, (n_q, features), 1)
    pieces = jnp.where(lane == 0, high, jnp.where(lane == 1, middle, jnp.where(lane == 2, low, 0.0)))
    wide_queries[:, :features] = (-2.0 * wide).astype(BF16)
    wide_queries[:, features:] = pieces.astype(BF16)
    lane = lax.broadcasted_iota(jnp.int32, ones.shape, 1)
    ones[...] = jnp.where(lane < 3, 1.0, 0.0).astype(BF16)
    total[...] = jnp.zeros_like(total)
    own_pattern.wait()

    for direction in (0, 1):
        z_copy(direction, 0).wait_recv()

        @pl.when(sends[direction])
        def _():
            z_copy(direction, 1).start()
            for part in range(CHUNKS // 2, CHUNKS):
                coef_copy(direction, 0, part).start()

        for distance in (1, 2):
            spread(1 + direction, distance)
    for slot in range(3):
        relay(slot)
    gathered(0)

    def evaluate(slot):
        place = 2 + jnp.where(slot % 2 == 1, -1, 1) * ((slot + 1) // 2)
        listed = pattern[place, pb].astype(F32)
        top = listed * (5.0 / radius ** 4)
        slope = listed * (4.0 / radius ** 5)
        points = centres[:, slot].reshape(share, features)
        point_wide = points.astype(F32)
        square = point_wide * point_wide
        square_high = square.astype(BF16)
        square_low = (square - square_high.astype(F32)).astype(BF16)
        point_norm = lax.dot_general(
            jnp.ones((8, 2 * features), BF16), jnp.concatenate([square_high, square_low], axis=1),
            (((1,), (1,)), ((), ())), preferred_element_type=F32,
        )
        right = jnp.concatenate([points, ones[...]], axis=1)

        @pl.loop(0, 2)
        def _(tile):
            span = pl.ds(pl.multiple_of(tile * half, half), half)
            cross = lax.dot_general(
                wide_queries[span, :], right, (((1,), (1,)), ((), ())), preferred_element_type=F32
            )
            sq_dist = (cross.reshape(half // 8, 8, share) + point_norm[None]).reshape(half, share)
            kern[core, slot, span, :] = wendland(sq_dist, radius, top, slope)

            @pl.when(tile == 1)
            def _():
                kern_copy(slot, 0).start()

            @pl.when((tile == 0) & (slot > 0))
            def _():
                kern_copy(slot - 1, 1).start()

    def product(slot, first, n_parts):
        owners = n_y // CHUNKS * n_parts
        start = first * (n_y // CHUNKS)
        columns = pl.ds(pl.multiple_of(start * rows, 128), owners * rows)
        left = jnp.concatenate([kern[c, slot, :, columns] for c in (0, 1)], axis=1)
        right = jnp.concatenate(
            [
                coefs[slot, pl.ds(pl.multiple_of((start + k) * 2 * rows + c * rows, rows), rows), :]
                for c in (0, 1) for k in range(owners)
            ],
            axis=0,
        )
        return jnp.dot(left, right, preferred_element_type=F32)

    @pl.loop(0, 6)
    def _(slot):
        @pl.when(slot == 1)
        def _():
            forward(0)
            for direction in (0, 1):
                z_copy(direction, 1).wait_recv()
                for distance in (1, 2):
                    spread(3 + direction, distance)
            forward(1)

        @pl.when(slot == 2)
        def _():
            forward(2)

        @pl.when(slot == 3)
        def _():
            for late in (3, 4):
                relay(late)
            forward(3)

        @pl.when(slot > 2)
        def _():
            kern_arrived(slot - 3)
            total[...] += product(slot - 3, 0, CHUNKS)

        for k in range(1, 5):
            @pl.when(slot == k)
            def _():
                gathered(k)

        @pl.when(slot < 5)
        def _():
            evaluate(slot)

    def far_coefs(direction, parts):
        for part in parts:
            coef_copy(direction, 1, part).wait_recv()

    early = CHUNKS // 2
    kern_copy(4, 1).start()
    kern_arrived(3)
    far_coefs(0, range(early))
    total[...] += product(3, 0, early)
    kern_arrived(4)
    far_coefs(1, range(early))
    total[...] += product(4, 0, early)
    for part in range(early, CHUNKS):
        for direction in (0, 1):
            far_coefs(direction, (part,))
        partial = product(3, part, 1) + product(4, part, 1)
        if part < CHUNKS - 1:
            total[...] += partial
        else:
            out_ref[...] = (total[...] + partial).astype(BF16)

    for direction in (0, 1):
        @pl.when(sends[direction])
        def _():
            for hop in (0, 1):
                z_copy(direction, hop).wait_send()
                for part in range(CHUNKS):
                    coef_copy(direction, hop, part).wait_send()

    for slot in range(5):
        for direction in (0, 1):
            for distance in range(1, farthest(slot, direction) + 1):
                y_copy(slot, direction, distance).wait_send()
    for slot in range(5):
        for tile in (0, 1):
            kern_copy(slot, tile).wait_send()


def per_device(n_pb, n_ao, queries, centres, coefs, pattern):
    n_q, features = queries.shape
    n_c, columns = coefs.shape
    rows = centres.shape[0]
    in_hbm = pl.BlockSpec(memory_space=pltpu.HBM)
    n_y = n_ao // 2
    dma = pltpu.SemaphoreType.DMA
    return pl.pallas_call(
        functools.partial(kernel, n_pb, n_ao),
        out_shape=jax.ShapeDtypeStruct((n_q, columns), BF16),
        in_specs=[in_hbm] * 4,
        out_specs=pl.BlockSpec(memory_space=pltpu.VMEM),
        scratch_shapes=[
            pltpu.VMEM((n_q, features), BF16),
            pltpu.VMEM((n_q, 2 * features), BF16),
            pltpu.VMEM((n_y * rows, features), BF16),
            pltpu.VMEM((n_y, 5, rows, features), BF16),
            pltpu.VMEM((5, n_c, columns), BF16),
            pltpu.VMEM((2, 5, n_q, n_c // 2), BF16),
            pltpu.VMEM((n_q, columns), F32),
            pltpu.SMEM(pattern.shape[::-1], jnp.int32),
            dma((4,)),
            pltpu.SemaphoreType.REGULAR,
            pltpu.SemaphoreType.REGULAR((2,)),
            dma((2, 2)), dma((2, 2)),
            dma((5, 2, n_y // 2)), dma((5, 2, n_y // 2)),
            dma((5, 2)), dma((5, 2)),
            dma((2, 2, CHUNKS)), dma((2, 2, CHUNKS)),
        ],
        compiler_params=pltpu.CompilerParams(
            collective_id=0, has_side_effects=True, vmem_limit_bytes=36 * 2 ** 20
        ),
    )(*[pltpu.with_memory_space_constraint(x, pltpu.HBM) for x in (queries, centres, coefs, pattern.T)])


def solution(mesh):
    in_specs = (P("pb", None), P(("pb", "ao"), None), P("pb", "ao"), P())
    out_specs = P("pb", "ao")
    return jax.shard_map(
        functools.partial(per_device, mesh.shape["pb"], mesh.shape["ao"]),
        mesh=mesh, in_specs=in_specs, out_specs=out_specs, check_vma=False,
    )
```

```python
import functools
import math

import jax
import jax.numpy as jnp
from jax import lax
from jax.experimental import pallas as pl
from jax.experimental.pallas import tpu as pltpu
from jax.sharding import PartitionSpec as P

RADIUS_FACTOR = 1.3
MESH = pl.DeviceIdType.MESH
F32 = jnp.float32
BF16 = jnp.bfloat16

OFFSETS = (0, -1, 1, -2, 2)
CHUNKS = 4


def wendland(sq_dist, radius, high, low):
    clamped = jnp.maximum(sq_dist, 1e-30)
    inner = jnp.maximum(radius - clamped * lax.rsqrt(clamped), 0.0)
    square = inner * inner
    return ((square * square) * (high - low * inner)).astype(BF16)


def kernel(
    n_pb, n_ao,
    queries_hbm, centres_hbm, coefs_hbm, pattern_hbm, out_ref,
    queries, wide_queries, ones, centres, coefs, kern, total, pattern,
    local_sem, ready, far, zs, zr, ys, yr, ss, sr, ks, kr,
):
    n_y = n_ao // 2
    n_q, features = queries.shape
    rows = centres.shape[2]
    block = coefs.shape[1]
    chunk = block // CHUNKS
    share = n_y * rows
    half = n_q // 2
    radius = RADIUS_FACTOR * math.sqrt(features)

    pb = lax.axis_index("pb")
    ao = lax.axis_index("ao")
    y = ao // 2
    core = ao % 2
    sibling = (pb, y * 2 + (1 - core))
    def y_peer(d):
        return (pb, lax.rem(y + d, n_y) * 2 + core)

    def pb_peer(shift):
        return (lax.rem(pb + shift + n_pb, n_pb), ao)

    has_below = pb > 0
    has_above = pb < n_pb - 1
    sends = (has_above, has_below)
    receives = (has_below, has_above)

    barrier = pltpu.get_barrier_semaphore()
    for peer in (y_peer(1), y_peer(n_y - 1), sibling):
        pl.semaphore_signal(barrier, inc=1, device_id=peer, device_id_type=MESH)

    @pl.when(has_below)
    def _():
        pl.semaphore_signal(barrier, inc=1, device_id=pb_peer(-1), device_id_type=MESH)

    own_centres = pltpu.make_async_copy(centres_hbm, centres.at[y, 0], local_sem.at[0])
    own_coefs = pltpu.make_async_copy(coefs_hbm, coefs.at[0], local_sem.at[1])
    own_queries = pltpu.make_async_copy(queries_hbm, queries, local_sem.at[2])
    own_pattern = pltpu.make_async_copy(pattern_hbm, pattern, local_sem.at[3])
    own_centres.start()
    own_coefs.start()
    own_queries.start()
    own_pattern.start()

    def remote(src, dst, send_sem, recv_sem, device):
        return pltpu.make_async_remote_copy(
            src_ref=src, dst_ref=dst, send_sem=send_sem, recv_sem=recv_sem,
            device_id=device, device_id_type=MESH,
        )

    def z_copy(direction, hop):
        src = 0 if hop == 0 else 1 + direction
        return remote(
            centres.at[y, src], centres.at[y, 1 + 2 * hop + direction],
            zs.at[direction, hop], zr.at[direction, hop], pb_peer(1 - 2 * direction),
        )

    def coef_copy(direction, hop, part):
        src = 0 if hop == 0 else 1 + direction
        span = pl.ds(part * chunk, chunk)
        return remote(
            coefs.at[src, span], coefs.at[1 + 2 * hop + direction, span],
            ks.at[direction, hop, part], kr.at[direction, hop, part], pb_peer(1 - 2 * direction),
        )

    def y_copy(slot, direction, distance, arriving=False):
        behind = distance if arriving else (0 if distance < 3 else 2)
        hops = distance if distance < 3 else distance - 2
        sign = 1 - 2 * direction
        view = centres.at[lax.rem(y + n_y - sign * behind, n_y), slot]
        return remote(
            view, view, ys.at[slot, direction, distance - 1], yr.at[slot, direction, distance - 1],
            y_peer(n_y + sign * hops),
        )

    def farthest(slot, direction):
        return n_y // 2 if direction == slot % 2 else n_y // 2 - 1

    def kern_copy(slot, tile, arriving=False):
        view = kern.at[1 - core if arriving else core, slot, pl.ds(pl.multiple_of(tile * half, half), half)]
        return remote(view, view, ss.at[slot, tile], sr.at[slot, tile], sibling)

    def kern_arrived(slot):
        for tile in (0, 1):
            kern_copy(slot, tile, arriving=True).wait_recv()

    def spread(slot, distance):
        for direction in (0, 1):
            y_copy(slot, direction, distance).start()

    def relay(slot):
        for direction in (0, 1):
            y_copy(slot, direction, 2, arriving=True).wait_recv()
            for distance in range(3, farthest(slot, direction) + 1):
                y_copy(slot, direction, distance).start()

    def gathered(slot):
        for direction in (0, 1):
            for distance in range(1, farthest(slot, direction) + 1):
                if distance != 2:
                    y_copy(slot, direction, distance, arriving=True).wait_recv()

    def forward(part):
        for direction in (0, 1):
            coef_copy(direction, 0, part).wait_recv()

            @pl.when(sends[direction])
            def _():
                coef_copy(direction, 1, part).start()

    for direction in (0, 1):
        @pl.when(jnp.logical_not(receives[direction]))
        def _():
            for hop in (0, 1):
                slot = 1 + 2 * hop + direction
                pltpu.make_async_copy(centres_hbm, centres.at[y, slot], zr.at[direction, hop]).start()
                for part in range(CHUNKS):
                    span = pl.ds(part * chunk, chunk)
                    pltpu.make_async_copy(
                        coefs_hbm.at[span], coefs.at[slot, span], kr.at[direction, hop, part]
                    ).start()

    own_centres.wait()
    own_coefs.wait()
    pl.semaphore_wait(barrier, 3 + has_above.astype(jnp.int32))

    @pl.when(has_above)
    def _():
        pl.semaphore_signal(ready, inc=1, device_id=pb_peer(1), device_id_type=MESH)
        z_copy(0, 0).start()
        coef_copy(0, 0, 0).start()

    spread(0, 1)
    for direction in (0, 1):
        pl.semaphore_signal(
            far.at[direction], inc=1, device_id=y_peer(n_y - 1 + 2 * direction), device_id_type=MESH
        )

    @pl.when(has_below)
    def _():
        pl.semaphore_wait(ready, 1)
        z_copy(1, 0).start()
        coef_copy(1, 0, 0).start()

    for direction in (0, 1):
        pl.semaphore_wait(far.at[direction], 1)
    spread(0, 2)

    own_queries.wait()
    wide = queries[...].astype(F32)
    norm = jnp.sum(wide * wide, axis=1, keepdims=True)
    high = norm.astype(BF16).astype(F32)
    middle = (norm - high).astype(BF16).astype(F32)
    low = norm - high - middle
    lane = lax.broadcasted_iota(jnp.int32, (n_q, features), 1)
    pieces = jnp.where(lane == 0, high, jnp.where(lane == 1, middle, jnp.where(lane == 2, low, 0.0)))
    wide_queries[:, :features] = (-2.0 * wide).astype(BF16)
    wide_queries[:, features:] = pieces.astype(BF16)
    lane = lax.broadcasted_iota(jnp.int32, ones.shape, 1)
    ones[...] = jnp.where(lane < 3, 1.0, 0.0).astype(BF16)
    total[...] = jnp.zeros_like(total)
    own_pattern.wait()

    for direction in (0, 1):
        z_copy(direction, 0).wait_recv()

        @pl.when(sends[direction])
        def _():
            z_copy(direction, 1).start()
            for part in range(1, CHUNKS):
                coef_copy(direction, 0, part).start()

        for distance in (1, 2):
            spread(1 + direction, distance)
    relay(0)
    for direction in (0, 1):
        z_copy(direction, 1).wait_recv()
        for distance in (1, 2):
            spread(3 + direction, distance)
    for slot in (1, 2):
        relay(slot)
    gathered(0)

    def evaluate(slot):
        place = 2 + jnp.where(slot % 2 == 1, -1, 1) * ((slot + 1) // 2)
        listed = pattern[place, pb].astype(F32)
        top = listed * (5.0 / radius ** 4)
        slope = listed * (4.0 / radius ** 5)
        points = centres[:, slot].reshape(share, features)
        point_wide = points.astype(F32)
        square = point_wide * point_wide
        square_high = square.astype(BF16)
        square_low = (square - square_high.astype(F32)).astype(BF16)
        point_norm = lax.dot_general(
            jnp.ones((8, 2 * features), BF16), jnp.concatenate([square_high, square_low], axis=1),
            (((1,), (1,)), ((), ())), preferred_element_type=F32,
        )
        right = jnp.concatenate([points, ones[...]], axis=1)

        @pl.loop(0, 2)
        def _(tile):
            span = pl.ds(pl.multiple_of(tile * half, half), half)
            cross = lax.dot_general(
                wide_queries[span, :], right, (((1,), (1,)), ((), ())), preferred_element_type=F32
            )
            sq_dist = (cross.reshape(half // 8, 8, share) + point_norm[None]).reshape(half, share)
            kern[core, slot, span, :] = wendland(sq_dist, radius, top, slope)

            @pl.when(tile == 1)
            def _():
                kern_copy(slot, 0).start()

            @pl.when((tile == 0) & (slot > 0))
            def _():
                kern_copy(slot - 1, 1).start()

    def product(slot, first, n_parts):
        owners = n_y // CHUNKS * n_parts
        start = first * (n_y // CHUNKS)
        columns = pl.ds(pl.multiple_of(start * rows, 128), owners * rows)
        left = jnp.concatenate([kern[c, slot, :, columns] for c in (0, 1)], axis=1)
        right = jnp.concatenate(
            [
                coefs[slot, pl.ds(pl.multiple_of((start + k) * 2 * rows + c * rows, rows), rows), :]
                for c in (0, 1) for k in range(owners)
            ],
            axis=0,
        )
        return jnp.dot(left, right, preferred_element_type=F32)

    @pl.loop(0, 6)
    def _(slot):
        @pl.when(slot == 1)
        def _():
            forward(0)
            for late in (3, 4):
                relay(late)
            forward(1)

        @pl.when(slot == 2)
        def _():
            forward(2)

        @pl.when(slot == 3)
        def _():
            forward(3)

        @pl.when(slot > 2)
        def _():
            kern_arrived(slot - 3)
            total[...] += product(slot - 3, 0, CHUNKS)

        for k in range(1, 5):
            @pl.when(slot == k)
            def _():
                gathered(k)

        @pl.when(slot < 5)
        def _():
            evaluate(slot)

    def far_coefs(direction, parts):
        for part in parts:
            coef_copy(direction, 1, part).wait_recv()

    early = CHUNKS // 2
    kern_copy(4, 1).start()
    kern_arrived(3)
    far_coefs(0, range(early))
    total[...] += product(3, 0, early)
    kern_arrived(4)
    far_coefs(1, range(early))
    total[...] += product(4, 0, early)
    for part in range(early, CHUNKS):
        for direction in (0, 1):
            far_coefs(direction, (part,))
        partial = product(3, part, 1) + product(4, part, 1)
        if part < CHUNKS - 1:
            total[...] += partial
        else:
            out_ref[...] = (total[...] + partial).astype(BF16)

    for direction in (0, 1):
        @pl.when(sends[direction])
        def _():
            for hop in (0, 1):
                z_copy(direction, hop).wait_send()
                for part in range(CHUNKS):
                    coef_copy(direction, hop, part).wait_send()

    for slot in range(5):
        for direction in (0, 1):
            for distance in range(1, farthest(slot, direction) + 1):
                y_copy(slot, direction, distance).wait_send()
    for slot in range(5):
        for tile in (0, 1):
            kern_copy(slot, tile).wait_send()


def per_device(n_pb, n_ao, queries, centres, coefs, pattern):
    n_q, features = queries.shape
    n_c, columns = coefs.shape
    rows = centres.shape[0]
    in_hbm = pl.BlockSpec(memory_space=pltpu.HBM)
    n_y = n_ao // 2
    dma = pltpu.SemaphoreType.DMA
    return pl.pallas_call(
        functools.partial(kernel, n_pb, n_ao),
        out_shape=jax.ShapeDtypeStruct((n_q, columns), BF16),
        in_specs=[in_hbm] * 4,
        out_specs=pl.BlockSpec(memory_space=pltpu.VMEM),
        scratch_shapes=[
            pltpu.VMEM((n_q, features), BF16),
            pltpu.VMEM((n_q, 2 * features), BF16),
            pltpu.VMEM((n_y * rows, features), BF16),
            pltpu.VMEM((n_y, 5, rows, features), BF16),
            pltpu.VMEM((5, n_c, columns), BF16),
            pltpu.VMEM((2, 5, n_q, n_c // 2), BF16),
            pltpu.VMEM((n_q, columns), F32),
            pltpu.SMEM(pattern.shape[::-1], jnp.int32),
            dma((4,)),
            pltpu.SemaphoreType.REGULAR,
            pltpu.SemaphoreType.REGULAR((2,)),
            dma((2, 2)), dma((2, 2)),
            dma((5, 2, n_y // 2)), dma((5, 2, n_y // 2)),
            dma((5, 2)), dma((5, 2)),
            dma((2, 2, CHUNKS)), dma((2, 2, CHUNKS)),
        ],
        compiler_params=pltpu.CompilerParams(
            collective_id=0, has_side_effects=True, vmem_limit_bytes=36 * 2 ** 20
        ),
    )(*[pltpu.with_memory_space_constraint(x, pltpu.HBM) for x in (queries, centres, coefs, pattern.T)])


def solution(mesh):
    in_specs = (P("pb", None), P(("pb", "ao"), None), P("pb", "ao"), P())
    out_specs = P("pb", "ao")
    return jax.shard_map(
        functools.partial(per_device, mesh.shape["pb"], mesh.shape["ao"]),
        mesh=mesh, in_specs=in_specs, out_specs=out_specs, check_vma=False,
    )
```

```python
import functools
import math

import jax
import jax.numpy as jnp
from jax import lax
from jax.experimental import pallas as pl
from jax.experimental.pallas import tpu as pltpu
from jax.sharding import PartitionSpec as P

RADIUS_FACTOR = 1.3
MESH = pl.DeviceIdType.MESH
F32 = jnp.float32
BF16 = jnp.bfloat16

OFFSETS = (0, -1, 1, -2, 2)
CHUNKS = 4


def wendland(sq_dist, radius, high, low):
    clamped = jnp.maximum(sq_dist, 1e-30)
    inner = jnp.maximum(radius - clamped * lax.rsqrt(clamped), 0.0)
    square = inner * inner
    return ((square * square) * (high - low * inner)).astype(BF16)


def kernel(
    n_pb, n_ao,
    queries_hbm, centres_hbm, coefs_hbm, pattern_hbm, out_ref,
    queries, wide_queries, ones, centres, coefs, kern, total, pattern,
    local_sem, ready, far, zs, zr, ys, yr, ss, sr, ks, kr,
):
    n_y = n_ao // 2
    n_q, features = queries.shape
    rows = centres.shape[2]
    block = coefs.shape[1]
    chunk = block // CHUNKS
    share = n_y * rows
    half = n_q // 2
    radius = RADIUS_FACTOR * math.sqrt(features)

    pb = lax.axis_index("pb")
    ao = lax.axis_index("ao")
    y = ao // 2
    core = ao % 2
    sibling = (pb, y * 2 + (1 - core))
    def y_peer(d):
        return (pb, lax.rem(y + d, n_y) * 2 + core)

    def pb_peer(shift):
        return (lax.rem(pb + shift + n_pb, n_pb), ao)

    has_below = pb > 0
    has_above = pb < n_pb - 1
    sends = (has_above, has_below)
    receives = (has_below, has_above)

    barrier = pltpu.get_barrier_semaphore()
    for peer in (y_peer(1), y_peer(n_y - 1), sibling):
        pl.semaphore_signal(barrier, inc=1, device_id=peer, device_id_type=MESH)

    @pl.when(has_below)
    def _():
        pl.semaphore_signal(barrier, inc=1, device_id=pb_peer(-1), device_id_type=MESH)

    own_centres = pltpu.make_async_copy(centres_hbm, centres.at[y, 0], local_sem.at[0])
    own_coefs = pltpu.make_async_copy(coefs_hbm, coefs.at[0], local_sem.at[1])
    own_queries = pltpu.make_async_copy(queries_hbm, queries, local_sem.at[2])
    own_pattern = pltpu.make_async_copy(pattern_hbm, pattern, local_sem.at[3])
    own_centres.start()
    own_coefs.start()
    own_queries.start()
    own_pattern.start()

    def remote(src, dst, send_sem, recv_sem, device):
        return pltpu.make_async_remote_copy(
            src_ref=src, dst_ref=dst, send_sem=send_sem, recv_sem=recv_sem,
            device_id=device, device_id_type=MESH,
        )

    def z_copy(direction, hop):
        src = 0 if hop == 0 else 1 + direction
        return remote(
            centres.at[y, src], centres.at[y, 1 + 2 * hop + direction],
            zs.at[direction, hop], zr.at[direction, hop], pb_peer(1 - 2 * direction),
        )

    def coef_copy(direction, hop, part):
        src = 0 if hop == 0 else 1 + direction
        span = pl.ds(part * chunk, chunk)
        return remote(
            coefs.at[src, span], coefs.at[1 + 2 * hop + direction, span],
            ks.at[direction, hop, part], kr.at[direction, hop, part], pb_peer(1 - 2 * direction),
        )

    def y_copy(slot, direction, distance, arriving=False):
        behind = distance if arriving else (0 if distance < 3 else 2)
        hops = distance if distance < 3 else distance - 2
        sign = 1 - 2 * direction
        view = centres.at[lax.rem(y + n_y - sign * behind, n_y), slot]
        return remote(
            view, view, ys.at[slot, direction, distance - 1], yr.at[slot, direction, distance - 1],
            y_peer(n_y + sign * hops),
        )

    def farthest(slot, direction):
        return n_y // 2 if direction == slot % 2 else n_y // 2 - 1

    def kern_copy(slot, tile, arriving=False):
        view = kern.at[1 - core if arriving else core, slot, pl.ds(pl.multiple_of(tile * half, half), half)]
        return remote(view, view, ss.at[slot, tile], sr.at[slot, tile], sibling)

    def kern_arrived(slot):
        for tile in (0, 1):
            kern_copy(slot, tile, arriving=True).wait_recv()

    def spread(slot, distance):
        for direction in (0, 1):
            y_copy(slot, direction, distance).start()

    def relay(slot):
        for direction in (0, 1):
            y_copy(slot, direction, 2, arriving=True).wait_recv()
            for distance in range(3, farthest(slot, direction) + 1):
                y_copy(slot, direction, distance).start()

    def gathered(slot):
        for direction in (0, 1):
            for distance in range(1, farthest(slot, direction) + 1):
                if distance != 2:
                    y_copy(slot, direction, distance, arriving=True).wait_recv()

    def forward(part):
        for direction in (0, 1):
            coef_copy(direction, 0, part).wait_recv()

            @pl.when(sends[direction])
            def _():
                coef_copy(direction, 1, part).start()

    for direction in (0, 1):
        @pl.when(jnp.logical_not(receives[direction]))
        def _():
            for hop in (0, 1):
                slot = 1 + 2 * hop + direction
                pltpu.make_async_copy(centres_hbm, centres.at[y, slot], zr.at[direction, hop]).start()
                for part in range(CHUNKS):
                    span = pl.ds(part * chunk, chunk)
                    pltpu.make_async_copy(
                        coefs_hbm.at[span], coefs.at[slot, span], kr.at[direction, hop, part]
                    ).start()

    own_centres.wait()
    own_coefs.wait()
    pl.semaphore_wait(barrier, 3 + has_above.astype(jnp.int32))

    @pl.when(has_above)
    def _():
        pl.semaphore_signal(ready, inc=1, device_id=pb_peer(1), device_id_type=MESH)
        z_copy(0, 0).start()
        coef_copy(0, 0, 0).start()

    spread(0, 1)
    for direction in (0, 1):
        pl.semaphore_signal(
            far.at[direction], inc=1, device_id=y_peer(n_y - 1 + 2 * direction), device_id_type=MESH
        )

    @pl.when(has_below)
    def _():
        pl.semaphore_wait(ready, 1)
        z_copy(1, 0).start()
        coef_copy(1, 0, 0).start()

    for direction in (0, 1):
        pl.semaphore_wait(far.at[direction], 1)
    spread(0, 2)

    own_queries.wait()
    wide = queries[...].astype(F32)
    norm = jnp.sum(wide * wide, axis=1, keepdims=True)
    high = norm.astype(BF16).astype(F32)
    middle = (norm - high).astype(BF16).astype(F32)
    low = norm - high - middle
    lane = lax.broadcasted_iota(jnp.int32, (n_q, features), 1)
    pieces = jnp.where(lane == 0, high, jnp.where(lane == 1, middle, jnp.where(lane == 2, low, 0.0)))
    wide_queries[:, :features] = (-2.0 * wide).astype(BF16)
    wide_queries[:, features:] = pieces.astype(BF16)
    lane = lax.broadcasted_iota(jnp.int32, ones.shape, 1)
    ones[...] = jnp.where(lane < 3, 1.0, 0.0).astype(BF16)
    total[...] = jnp.zeros_like(total)
    own_pattern.wait()

    for direction in (0, 1):
        z_copy(direction, 0).wait_recv()

        @pl.when(sends[direction])
        def _():
            z_copy(direction, 1).start()
            for part in range(1, CHUNKS):
                coef_copy(direction, 0, part).start()

        for distance in (1, 2):
            spread(1 + direction, distance)
    relay(0)
    for direction in (0, 1):
        z_copy(direction, 1).wait_recv()
        for distance in (1, 2):
            spread(3 + direction, distance)
    for slot in (1, 2):
        relay(slot)
    gathered(0)

    def evaluate(slot):
        place = 2 + jnp.where(slot % 2 == 1, -1, 1) * ((slot + 1) // 2)
        listed = pattern[place, pb].astype(F32)
        top = listed * (5.0 / radius ** 4)
        slope = listed * (4.0 / radius ** 5)
        points = centres[:, slot].reshape(share, features)
        point_wide = points.astype(F32)
        square = point_wide * point_wide
        square_high = square.astype(BF16)
        square_low = (square - square_high.astype(F32)).astype(BF16)
        point_norm = lax.dot_general(
            jnp.ones((8, 2 * features), BF16), jnp.concatenate([square_high, square_low], axis=1),
            (((1,), (1,)), ((), ())), preferred_element_type=F32,
        )
        right = jnp.concatenate([points, ones[...]], axis=1)

        @pl.loop(0, 2)
        def _(tile):
            span = pl.ds(pl.multiple_of(tile * half, half), half)
            cross = lax.dot_general(
                wide_queries[span, :], right, (((1,), (1,)), ((), ())), preferred_element_type=F32
            )
            sq_dist = (cross.reshape(half // 8, 8, share) + point_norm[None]).reshape(half, share)
            kern[core, slot, span, :] = wendland(sq_dist, radius, top, slope)

            @pl.when(tile == 1)
            def _():
                kern_copy(slot, 0).start()

            @pl.when((tile == 0) & (slot > 0))
            def _():
                kern_copy(slot - 1, 1).start()

    def product(slot, first, n_parts):
        owners = n_y // CHUNKS * n_parts
        start = first * (n_y // CHUNKS)
        columns = pl.ds(pl.multiple_of(start * rows, 128), owners * rows)
        left = jnp.concatenate([kern[c, slot, :, columns] for c in (0, 1)], axis=1)
        right = jnp.concatenate(
            [
                coefs[slot, pl.ds(pl.multiple_of((start + k) * 2 * rows + c * rows, rows), rows), :]
                for c in (0, 1) for k in range(owners)
            ],
            axis=0,
        )
        return jnp.dot(left, right, preferred_element_type=F32)

    @pl.loop(0, 6)
    def _(slot):
        @pl.when(slot == 1)
        def _():
            forward(0)
            for late in (3, 4):
                relay(late)
            forward(1)

        @pl.when(slot == 2)
        def _():
            forward(2)

        @pl.when(slot == 3)
        def _():
            forward(3)

        @pl.when(slot > 2)
        def _():
            kern_arrived(slot - 3)
            total[...] += product(slot - 3, 0, CHUNKS)

        for k in range(1, 5):
            @pl.when(slot == k)
            def _():
                gathered(k)

        @pl.when(slot < 5)
        def _():
            evaluate(slot)

    def far_coefs(direction, parts):
        for part in parts:
            coef_copy(direction, 1, part).wait_recv()

    early = CHUNKS // 2
    kern_copy(4, 1).start()
    kern_arrived(3)
    far_coefs(0, range(early))
    total[...] += product(3, 0, early)
    kern_arrived(4)
    far_coefs(1, range(CHUNKS))
    total[...] += product(4, 0, CHUNKS)
    far_coefs(0, range(early, CHUNKS - 1))
    total[...] += product(3, early, CHUNKS - 1 - early)
    far_coefs(0, (CHUNKS - 1,))
    out_ref[...] = (total[...] + product(3, CHUNKS - 1, 1)).astype(BF16)

    for direction in (0, 1):
        @pl.when(sends[direction])
        def _():
            for hop in (0, 1):
                z_copy(direction, hop).wait_send()
                for part in range(CHUNKS):
                    coef_copy(direction, hop, part).wait_send()

    for slot in range(5):
        for direction in (0, 1):
            for distance in range(1, farthest(slot, direction) + 1):
                y_copy(slot, direction, distance).wait_send()
    for slot in range(5):
        for tile in (0, 1):
            kern_copy(slot, tile).wait_send()


def per_device(n_pb, n_ao, queries, centres, coefs, pattern):
    n_q, features = queries.shape
    n_c, columns = coefs.shape
    rows = centres.shape[0]
    in_hbm = pl.BlockSpec(memory_space=pltpu.HBM)
    n_y = n_ao // 2
    dma = pltpu.SemaphoreType.DMA
    return pl.pallas_call(
        functools.partial(kernel, n_pb, n_ao),
        out_shape=jax.ShapeDtypeStruct((n_q, columns), BF16),
        in_specs=[in_hbm] * 4,
        out_specs=pl.BlockSpec(memory_space=pltpu.VMEM),
        scratch_shapes=[
            pltpu.VMEM((n_q, features), BF16),
            pltpu.VMEM((n_q, 2 * features), BF16),
            pltpu.VMEM((n_y * rows, features), BF16),
            pltpu.VMEM((n_y, 5, rows, features), BF16),
            pltpu.VMEM((5, n_c, columns), BF16),
            pltpu.VMEM((2, 5, n_q, n_c // 2), BF16),
            pltpu.VMEM((n_q, columns), F32),
            pltpu.SMEM(pattern.shape[::-1], jnp.int32),
            dma((4,)),
            pltpu.SemaphoreType.REGULAR,
            pltpu.SemaphoreType.REGULAR((2,)),
            dma((2, 2)), dma((2, 2)),
            dma((5, 2, n_y // 2)), dma((5, 2, n_y // 2)),
            dma((5, 2)), dma((5, 2)),
            dma((2, 2, CHUNKS)), dma((2, 2, CHUNKS)),
        ],
        compiler_params=pltpu.CompilerParams(
            collective_id=0, has_side_effects=True, vmem_limit_bytes=36 * 2 ** 20
        ),
    )(*[pltpu.with_memory_space_constraint(x, pltpu.HBM) for x in (queries, centres, coefs, pattern.T)])


def solution(mesh):
    in_specs = (P("pb", None), P(("pb", "ao"), None), P("pb", "ao"), P())
    out_specs = P("pb", "ao")
    return jax.shard_map(
        functools.partial(per_device, mesh.shape["pb"], mesh.shape["ao"]),
        mesh=mesh, in_specs=in_specs, out_specs=out_specs, check_vma=False,
    )
```
